512 devices in a mesh: shard: 64 (over z, x), tensor: 4 (over y), section: 2 (over core).
Axes of the slice: x: 4, y: 4, z: 16, core: 2. Of those that a mesh axis runs over, the one named last changes fastest.
Arguments:
- query_key: float32 [2, 2, 1024, 1024], P('section', None, 'shard', 'tensor'), may hold values from -52 to 52, as said below
- query_key_gradient: float32 [2, 2, 1024, 1024], P('section', None, 'shard', 'tensor'), may hold values from -52 to 52
- query_key_first: float32 [2, 2, 1024, 1024], P('section', None, 'shard', 'tensor'), may hold values from -5.2 to 5.2
- query_key_second: float32 [2, 2, 1024, 1024], P('section', None, 'shard', 'tensor'), may hold values from 0.01 to 1
- value_gate: float32 [2, 2, 1024, 2048], P('section', None, 'shard', 'tensor'), may hold values from -52 to 52
- value_gate_gradient: float32 [2, 2, 1024, 2048], P('section', None, 'shard', 'tensor'), may hold values from -52 to 52
- value_gate_first: float32 [2, 2, 1024, 2048], P('section', None, 'shard', 'tensor'), may hold values from -5.2 to 5.2
- value_gate_second: float32 [2, 2, 1024, 2048], P('section', None, 'shard', 'tensor'), may hold values from 0.01 to 1
- output_weight: float32 [2, 2048, 1024], P('section', 'tensor', 'shard'), may hold values from -52 to 52
- output_gradient: float32 [2, 2048, 1024], P('section', 'tensor', 'shard'), may hold values from -52 to 52
- output_first: float32 [2, 2048, 1024], P('section', 'tensor', 'shard'), may hold values from -5.2 to 5.2
- output_second: float32 [2, 2048, 1024], P('section', 'tensor', 'shard'), may hold values from 0.01 to 1
- norm_gain: float32 [2, 1024], P('section', 'shard'), may hold values from -52 to 52
- gain_gradient: float32 [2, 1024], P('section', 'shard'), may hold values from -52 to 52
- gain_first: float32 [2, 1024], P('section', 'shard'), may hold values from -5.2 to 5.2
- gain_second: float32 [2, 1024], P('section', 'shard'), may hold values from 0.01 to 1
Outputs:
- new_query_key: float32 [2, 2, 1024, 1024], P('section', None, 'shard', 'tensor')
- new_query_key_first: float32 [2, 2, 1024, 1024], P('section', None, 'shard', 'tensor')
- new_query_key_second: float32 [2, 2, 1024, 1024], P('section', None, 'shard', 'tensor')
- new_value_gate: float32 [2, 2, 1024, 2048], P('section', None, 'shard', 'tensor')
- new_value_gate_first: float32 [2, 2, 1024, 2048], P('section', None, 'shard', 'tensor')
- new_value_gate_second: float32 [2, 2, 1024, 2048], P('section', None, 'shard', 'tensor')
- new_output: float32 [2, 2048, 1024], P('section', 'tensor', 'shard')
- new_output_first: float32 [2, 2048, 1024], P('section', 'tensor', 'shard')
- new_output_second: float32 [2, 2048, 1024], P('section', 'tensor', 'shard')
- new_gain: float32 [2, 1024], P('section', 'shard')
- new_gain_first: float32 [2, 1024], P('section', 'shard')
- new_gain_second: float32 [2, 1024], P('section', 'shard')
- copy_query_key: bfloat16 [2, 2, 1024, 1024], P('section', None, None, 'tensor')
- copy_value_gate: bfloat16 [2, 2, 1024, 2048], P('section', None, None, 'tensor')
- copy_output: bfloat16 [2, 2048, 1024], P('section', 'tensor')
- copy_gain: bfloat16 [2, 1024], P('section')
The draws below stay inside these ranges and needn't reach their ends.
Inputs may be any that keep to these rules, and one draw needn't show every extreme that they name: `query_key`: projection weights, gradients and first moments are real-valued with entries of differing scale.
All inputs are finite; a program needn't handle non-finite values.
Results may differ from the reference program's by a relative error of at most 0.001.
Values may be sent and summed in bfloat16 or wider, within the bound.
A program may use at most 64 MiB of HBM per device.

```python
import math
import jax
import jax.numpy as jnp
from jax import lax

D = 1024
VDIM = 2048
STEP = 10
LAYERS = 2


def scaled_draw(key, shape, rising, spread, factor):
    key_base, key_jitter, key_other = jax.random.split(key, 3)
    base = jnp.clip(jax.random.normal(key_base, shape, jnp.float32), -4.0, 4.0)
    count = shape[rising]
    position = jnp.arange(count, dtype=jnp.float32) / count
    rise_shape = [1] * len(shape)
    rise_shape[rising] = count
    rise = jnp.exp(math.log(10.0) * position).reshape(rise_shape)
    other_shape = [1] * len(shape)
    other_shape[spread] = shape[spread]
    other = jnp.exp(jax.random.uniform(key_other, (shape[spread],), jnp.float32, 0.0, math.log(10.0))).reshape(other_shape)
    jitter = jax.random.uniform(key_jitter, shape, jnp.float32, 0.7, 1.3)
    return base * rise * other * jitter * factor


def draw_query_key(key, part):
    return scaled_draw(jax.random.fold_in(key, 11), (LAYERS, 2, D, D), 2, 3, 0.1)


def draw_query_key_gradient(key, part):
    return scaled_draw(jax.random.fold_in(key, 12), (LAYERS, 2, D, D), 2, 3, 0.1)


def draw_query_key_first(key, part):
    return scaled_draw(jax.random.fold_in(key, 13), (LAYERS, 2, D, D), 2, 3, 0.01)


def draw_value_gate(key, part):
    return scaled_draw(jax.random.fold_in(key, 21), (LAYERS, 2, D, VDIM), 2, 3, 0.1)


def draw_value_gate_gradient(key, part):
    return scaled_draw(jax.random.fold_in(key, 22), (LAYERS, 2, D, VDIM), 2, 3, 0.1)


def draw_value_gate_first(key, part):
    return scaled_draw(jax.random.fold_in(key, 23), (LAYERS, 2, D, VDIM), 2, 3, 0.01)


def draw_output_weight(key, part):
    return scaled_draw(jax.random.fold_in(key, 31), (LAYERS, VDIM, D), 2, 1, 0.1)


def draw_output_gradient(key, part):
    return scaled_draw(jax.random.fold_in(key, 32), (LAYERS, VDIM, D), 2, 1, 0.1)


def draw_output_first(key, part):
    return scaled_draw(jax.random.fold_in(key, 33), (LAYERS, VDIM, D), 2, 1, 0.01)


def draw_norm_gain(key, part):
    return scaled_draw(jax.random.fold_in(key, 41), (LAYERS, D), 1, 0, 0.1)


def draw_gain_gradient(key, part):
    return scaled_draw(jax.random.fold_in(key, 42), (LAYERS, D), 1, 0, 0.1)


def draw_gain_first(key, part):
    return scaled_draw(jax.random.fold_in(key, 43), (LAYERS, D), 1, 0, 0.01)


def block_scale(rng, extent, shards, low, high):
    gain = 1.0
    for axis_at, shards_of in shards:
        draws = jax.random.uniform(jax.random.fold_in(jax.random.fold_in(rng, 6), axis_at), (shards_of,), jnp.float32, low / len(shards), high / len(shards))
        gain = gain * jnp.repeat(jnp.exp(draws), extent[axis_at] // shards_of).reshape((-1,) + (1,) * (len(extent) - 1 - axis_at))
    return gain


def setup_inputs(seed: int = 0) -> dict:
    key_list = jax.random.split(jax.random.key(seed), 17)
    query_key = draw_query_key(jax.random.fold_in(key_list[16], 71), 0)
    query_key_gradient = draw_query_key_gradient(jax.random.fold_in(key_list[16], 71), 0)
    query_key_first = draw_query_key_first(jax.random.fold_in(key_list[16], 71), 0)
    query_key_second = jnp.clip(jnp.exp(math.log(1.0) - 4.6051702 * jax.random.uniform(key_list[3], (LAYERS, 2, D, D), jnp.float32) ** block_scale(key_list[3], (LAYERS, 2, D, D), ((0, 2), (2, 64), (3, 4)), -0.2, 0.2)), 0.01, 1.0)
    value_gate = draw_value_gate(jax.random.fold_in(key_list[16], 71), 0)
    value_gate_gradient = draw_value_gate_gradient(jax.random.fold_in(key_list[16], 71), 0)
    value_gate_first = draw_value_gate_first(jax.random.fold_in(key_list[16], 71), 0)
    value_gate_second = jnp.clip(jnp.exp(math.log(1.0) - 4.6051702 * jax.random.uniform(key_list[7], (LAYERS, 2, D, VDIM), jnp.float32) ** block_scale(key_list[7], (LAYERS, 2, D, VDIM), ((0, 2), (2, 64), (3, 4)), -0.2, 0.2)), 0.01, 1.0)
    output_weight = draw_output_weight(jax.random.fold_in(key_list[16], 71), 0)
    output_gradient = draw_output_gradient(jax.random.fold_in(key_list[16], 71), 0)
    output_first = draw_output_first(jax.random.fold_in(key_list[16], 71), 0)
    output_second = jnp.clip(jnp.exp(math.log(1.0) - 4.6051702 * jax.random.uniform(key_list[11], (LAYERS, VDIM, D), jnp.float32) ** block_scale(key_list[11], (LAYERS, VDIM, D), ((0, 2), (1, 4), (2, 64)), -0.2, 0.2)), 0.01, 1.0)
    norm_gain = draw_norm_gain(jax.random.fold_in(key_list[16], 71), 0)
    gain_gradient = draw_gain_gradient(jax.random.fold_in(key_list[16], 71), 0)
    gain_first = draw_gain_first(jax.random.fold_in(key_list[16], 71), 0)
    gain_second = jnp.clip(jnp.exp(math.log(1.0) - 4.6051702 * jax.random.uniform(key_list[15], (LAYERS, D), jnp.float32) ** block_scale(key_list[15], (LAYERS, D), ((0, 2), (1, 64)), -0.2, 0.2)), 0.01, 1.0)
    return dict(query_key=query_key, query_key_gradient=query_key_gradient, query_key_first=query_key_first, query_key_second=query_key_second, value_gate=value_gate, value_gate_gradient=value_gate_gradient, value_gate_first=value_gate_first, value_gate_second=value_gate_second, output_weight=output_weight, output_gradient=output_gradient, output_first=output_first, output_second=output_second, norm_gain=norm_gain, gain_gradient=gain_gradient, gain_first=gain_first, gain_second=gain_second)


beta_one = 0.9
beta_two = 0.999
epsilon = 1e-06
learn_rate = 0.2

def lamb_update(weight, gradient, first, second, decay, matrix_dims):
    first_new = beta_one * first + (1.0 - beta_one) * gradient
    second_new = beta_two * second + (1.0 - beta_two) * gradient * gradient
    update = first_new / (1.0 - beta_one ** STEP) / (jnp.sqrt(second_new / (1.0 - beta_two ** STEP)) + epsilon) + decay * weight
    norm_axes = tuple(range(weight.ndim - matrix_dims, weight.ndim))
    weight_sq = lax.optimization_barrier(jnp.sum(weight * weight, axis=norm_axes))
    update_sq = lax.optimization_barrier(jnp.sum(update * update, axis=norm_axes))
    trust = jnp.sqrt(weight_sq) / (jnp.sqrt(update_sq) + epsilon)
    trust = trust.reshape(trust.shape + (1,) * matrix_dims)
    new_weight = weight - learn_rate * trust * update
    return (new_weight, first_new, second_new)

def reference(query_key, query_key_gradient, query_key_first, query_key_second, value_gate, value_gate_gradient, value_gate_first, value_gate_second, output_weight, output_gradient, output_first, output_second, norm_gain, gain_gradient, gain_first, gain_second):
    new_qk, qk_m, qk_s = lamb_update(query_key, query_key_gradient, query_key_first, query_key_second, 0.01, 2)
    new_vg, vg_m, vg_s = lamb_update(value_gate, value_gate_gradient, value_gate_first, value_gate_second, 0.01, 2)
    new_output, output_m, output_s = lamb_update(output_weight, output_gradient, output_first, output_second, 0.01, 2)
    new_gain, gain_m, gain_s = lamb_update(norm_gain, gain_gradient, gain_first, gain_second, 0.0, 1)
    return (new_qk, qk_m, qk_s, new_vg, vg_m, vg_s, new_output, output_m, output_s, new_gain, gain_m, gain_s, new_qk.astype(jnp.bfloat16), new_vg.astype(jnp.bfloat16), new_output.astype(jnp.bfloat16), new_gain.astype(jnp.bfloat16))
```

```python
import functools

import jax
import jax.numpy as jnp
from jax import lax
from jax.experimental import pallas as pl
from jax.experimental.pallas import tpu as pltpu
from jax.sharding import PartitionSpec as P

STEP = 10
BETA_ONE = 0.9
BETA_TWO = 0.999
EPSILON = 1e-06
LEARN_RATE = 0.2
FIRST_SCALE = 1.0 / (1.0 - BETA_ONE**STEP)
SECOND_SCALE = 1.0 / (1.0 - BETA_TWO**STEP)

MESH = pl.DeviceIdType.MESH
NX, NY, NZ = 4, 4, 16
HALF = NZ // 2
ROWS = 16
GROUP = NX * ROWS
A_COLS, B_COLS = 768, 1280
SUBS = 4
W_LANE, U_LANE = 64, 72
LAG = 1


def terms(p, g, m, s, decay):
    first = BETA_ONE * m + (1.0 - BETA_ONE) * g
    second = BETA_TWO * s + (1.0 - BETA_TWO) * g * g
    update = first * FIRST_SCALE / (jnp.sqrt(second * SECOND_SCALE) + EPSILON)
    if decay:
        update = update + decay * p
    return first, second, update


def total(v):
    return jnp.sum(jnp.sum(v, axis=0, keepdims=True), axis=1, keepdims=True)


def comm_kernel(*refs):
    (qk_p, qk_g, qk_m, qk_s, vg_p, vg_g, vg_m, vg_s, o_p, o_g, o_m, o_s, n_p, n_g, n_m, n_s) = refs[:16]
    (qk_new, qk_first, qk_second, vg_new, vg_first, vg_second, o_new, o_first, o_second,
     n_new, n_first, n_second, part_a, part_b, o_copy, n_copy) = refs[16:32]
    (b_qk, b_vg, b_o, b_n, u_qk, u_vg, u_o, slots_one, slots_two, load_sem, one_send, one_recv, two_send, two_recv,
     ax_send, ax_recv, bz_send, bz_recv, bx_send, bx_recv, br_send, br_recv, az_send, az_recv) = refs[32:]

    shard = lax.axis_index("shard")
    y = lax.axis_index("tensor")
    z = shard // NX
    x = shard % NX
    q = y * NX + x

    def at(dz=0, dx=0):
        return {"shard": ((z + dz + NZ) % NZ) * NX + (x + dx + NX) % NX}

    def at_plane(d):
        other = (q + d) % (NX * NY)
        return {"shard": z * NX + other % NX, "tensor": other // NX}

    def rows(dz=0, dx=0):
        return pl.multiple_of(((z + dz + NZ) % NZ) * GROUP + ((x + dx + NX) % NX) * ROWS, ROWS)

    barrier = pltpu.get_barrier_semaphore()
    for d in range(1, NX * NY):
        pl.semaphore_signal(barrier, inc=1, device_id=at_plane(d), device_id_type=MESH)
    for d in range(1, NZ):
        pl.semaphore_signal(barrier, inc=1, device_id=at(dz=d), device_id_type=MESH)

    loads = []
    for i, (group, buffer) in enumerate((
        ((qk_p, qk_g, qk_m, qk_s), b_qk), ((vg_p, vg_g, vg_m, vg_s), b_vg),
        ((o_p, o_g, o_m, o_s), b_o), ((n_p, n_g, n_m, n_s), b_n))):
        for k, ref in enumerate(group):
            loads.append(pltpu.make_async_copy(ref, buffer.at[k], load_sem.at[4 * i + k]))
            loads[-1].start()

    lane = lax.broadcasted_iota(jnp.int32, (1, 128), 1)
    line = jnp.zeros((1, 128), jnp.float32)
    for k in range(4):
        loads[12 + k].wait()
    first, second, gain_update = terms(b_n[0], b_n[1], b_n[2], b_n[3], 0.0)
    n_first[...] = first
    n_second[...] = second
    slots_one[q] = line
    slots_one[q, :, 0:16] = b_n[0]
    slots_one[q, :, 16:32] = gain_update
    index = 0
    for i, (buffer, u_ref, first_ref, second_ref, count) in enumerate((
        (b_qk, u_qk, qk_first, qk_second, 2), (b_vg, u_vg, vg_first, vg_second, 2), (b_o, u_o, o_first, o_second, 1))):
        for k in range(4):
            loads[4 * i + k].wait()
        for k in range(count):
            p, g, m, s = (buffer[j, k] for j in range(4))
            first, second, update = terms(p, g, m, s, 0.01)
            first_ref[k] = first
            second_ref[k] = second
            u_ref[k] = update
            line = jnp.where(lane == W_LANE + index, total(p * p), line)
            line = jnp.where(lane == U_LANE + index, total(update * update), line)
            index += 1
    slots_one[q] = slots_one[q] + line

    pl.semaphore_wait(barrier, NX * NY - 1 + NZ - 1)
    sends = []
    one = []
    for d in range(1, NX * NY):
        one.append(pltpu.make_async_remote_copy(
            slots_one.at[q], slots_one.at[q], one_send.at[d - 1], one_recv.at[d - 1], device_id=at_plane(d), device_id_type=MESH))
        one[-1].start()
    for copy in one:
        copy.wait_recv()
    sends += one
    plane = slots_one[0]
    for d in range(1, NX * NY):
        plane = plane + slots_one[d]
    gains = jnp.zeros((1, 128), jnp.float32)
    for k in range(NX):
        gain_line = jnp.where(lane < 32, slots_one[y * NX + k], 0.0)
        gains = gains + (pltpu.roll(gain_line, 32 * k, 1) if k else gain_line)
    slots_two[z, 0:1] = plane
    slots_two[z, 1:2] = gains
    two = []
    for d in range(1, NZ):
        two.append(pltpu.make_async_remote_copy(
            slots_two.at[z], slots_two.at[z], two_send.at[d - 1], two_recv.at[d - 1], device_id=at(dz=d), device_id_type=MESH))
        two[-1].start()
    for copy in two:
        copy.wait_recv()
    sends += two
    sums = slots_two[0, 0:1]
    for d in range(1, NZ):
        sums = sums + slots_two[d, 0:1]
    roots = jnp.sqrt(jnp.where(lane >= W_LANE, sums, 0.0))
    ratio = LEARN_RATE * (roots / (pltpu.roll(roots, 128 - (U_LANE - W_LANE), 1) + EPSILON))
    rate = [jnp.sum(jnp.where(lane == W_LANE + i, ratio, 0.0), axis=1, keepdims=True) for i in range(5)]

    mine = rows()
    new = b_vg[0, 0] - rate[2] * u_vg[0]
    vg_new[0] = new
    part_b[pl.ds(mine, ROWS), 0:512] = new.astype(jnp.bfloat16)
    new = b_vg[0, 1] - rate[3] * u_vg[1]
    vg_new[1] = new
    part_b[pl.ds(mine, ROWS), 512:1024] = new.astype(jnp.bfloat16)
    new = b_qk[0, 1] - rate[1] * u_qk[1]
    qk_new[1] = new
    part_b[pl.ds(mine, ROWS), 1024:1280] = new.astype(jnp.bfloat16)

    def send(ref, start, size, send_sem, recv_sem, target):
        block = ref.at[pl.ds(start, size)]
        copy = pltpu.make_async_remote_copy(block, block, send_sem, recv_sem, device_id=target, device_id_type=MESH)
        copy.start()
        sends.append(copy)
        return copy

    SIDE = (1, -1)
    STEPS = (HALF, HALF - 1)

    def send_bz(side, k):
        return send(part_b, rows(dz=-SIDE[side] * k), ROWS, bz_send.at[side, k], bz_recv.at[side, k], at(dz=SIDE[side]))

    def send_bx(j, dz):
        return [send(part_b, rows(dz=dz), ROWS, bx_send.at[side, j], bx_recv.at[side, j], at(dx=SIDE[side])) for side in range(2)]

    def relay_bx(j, dz):
        side = j % 2
        across[j][side].wait_recv()
        return send(part_b, rows(dz=dz, dx=-SIDE[side]), ROWS, br_send.at[j], br_recv.at[j], at(dx=SIDE[side]))

    PIECE = GROUP // SUBS

    def subs_of(side, k):
        if k < HALF - 1:
            return range(SUBS)
        return range(SUBS // 2) if side == 0 else range(SUBS // 2, SUBS)

    def send_az(side, k, h):
        dz = -SIDE[side] * k
        start = pl.multiple_of(((z + dz + NZ) % NZ) * GROUP + h * PIECE, PIECE)
        return send(part_a, start, PIECE, az_send.at[side, k, h], az_recv.at[side, k, h], at(dz=SIDE[side]))

    bz = [[send_bz(0, 0)], [send_bz(1, 0)]]
    new = b_o[0, 0] - rate[4] * u_o[0]
    o_new[0] = new
    part_a[pl.ds(mine, ROWS), 0:512] = new.astype(jnp.bfloat16)
    new = b_qk[0, 0] - rate[0] * u_qk[0]
    qk_new[0] = new
    part_a[pl.ds(mine, ROWS), 512:768] = new.astype(jnp.bfloat16)
    ax = [send(part_a, mine, ROWS, ax_send.at[d - 1], ax_recv.at[d - 1], at(dx=d)) for d in (1, 3, 2)]
    across = {0: send_bx(0, 0)}
    relays = {}
    where = {0: 0}

    lanes = lax.broadcasted_iota(jnp.int32, (NZ, 128), 1)
    held = jnp.concatenate([slots_two[d, 1:2] for d in range(NZ)], axis=0)
    valid = lanes % 32 < 16
    gain = jnp.where(valid, held, 0.0)
    update = jnp.where(valid, pltpu.roll(held, 128 - 16, 1), 0.0)
    gain_rate = LEARN_RATE * (jnp.sqrt(total(gain * gain)) / (jnp.sqrt(total(update * update)) + EPSILON))
    n_new[...] = b_n[0] - gain_rate * gain_update
    gain = gain - gain_rate * update
    packed = jnp.where(lanes < 16, gain, 0.0)
    for k in range(1, NX):
        packed = packed + jnp.where((lanes >= 16 * k) & (lanes < 16 * k + 16), pltpu.roll(gain, 128 - 16 * k, 1), 0.0)
    moved = pltpu.roll(packed, 64, 1)
    for d in range(HALF):
        n_copy[:, 128 * d : 128 * d + 128] = (packed[2 * d : 2 * d + 1] + moved[2 * d + 1 : 2 * d + 2]).astype(jnp.bfloat16)

    def transpose_pair(i):
        start = pl.multiple_of((z // 2 + i + HALF) % HALF * 128, 128)
        block = part_a[pl.ds(start, 128), 0:512].astype(jnp.float32)
        o_copy[:, pl.ds(start, 128)] = block.T.astype(jnp.bfloat16)

    az = [{}, {}]

    def az_step(k):
        if k == 0:
            for copy in ax:
                copy.wait_recv()
        for h in range(SUBS):
            for side in range(2):
                if k:
                    if h in subs_of(side, k - 1):
                        az[side][k - 1, h].wait_recv()
                if k < HALF and h in subs_of(side, k):
                    az[side][k, h] = send_az(side, k, h)
        if k == HALF:
            transpose_pair(HALF // 2)
        elif k % 2 == 1:
            i = (k - 1) // 2
            transpose_pair(-i)
            if i:
                transpose_pair(i)

    for k in range(HALF + max(LAG, 1) + 1):
        if k < HALF:
            for side in range(2):
                if k < STEPS[side]:
                    bz[side][k].wait_recv()
                    if k + 1 < STEPS[side]:
                        bz[side].append(send_bz(side, k + 1))
                    j = 1 + 2 * k + side
                    where[j] = -SIDE[side] * (k + 1)
                    across[j] = send_bx(j, where[j])
        if k >= LAG and k - LAG <= HALF:
            az_step(k - LAG)
        for j in ((0,) if k == 0 else (2 * k - 1, 2 * k)):
            if j < NZ:
                relays[j] = relay_bx(j, where[j])
    for j in range(NZ):
        across[j][1 - j % 2].wait_recv()
        relays[j].wait_recv()
    for copy in sends:
        copy.wait_send()


def store_kernel(*refs):
    (qk_new, qk_first, qk_second, vg_new, vg_first, vg_second, o_new, o_first, o_second,
     n_new, n_first, n_second, part_a, part_b, o_copy, n_copy) = refs[:16]
    outs = refs[16:32]
    sem = refs[32]
    pairs = [
        (part_b.at[:, 0:512], outs[13].at[0]), (part_b.at[:, 512:1024], outs[13].at[1]), (o_copy, outs[14]),
        (part_a.at[:, 512:768], outs[12].at[0]), (part_b.at[:, 1024:1280], outs[12].at[1]),
        *zip(refs[:12], outs[:12]), (n_copy, outs[15])]
    copies = [pltpu.make_async_copy(source, target, sem.at[i]) for i, (source, target) in enumerate(pairs)]
    for copy in copies:
        copy.start()
    for copy in copies:
        copy.wait()


def on_device(*args):
    f32, bf16 = jnp.float32, jnp.bfloat16
    operands = []
    for i, array in enumerate(args):
        if i < 8:
            operands.append(array.reshape(array.shape[1:]))
        elif i < 12:
            operands.append(jnp.swapaxes(array, 1, 2))
        else:
            operands.append(array)
    qk, vg, o, n = (operands[4 * i].shape for i in range(4))
    small = [(qk, f32)] * 3 + [(vg, f32)] * 3 + [(o, f32)] * 3 + [(n, f32)] * 3
    rows = NZ * GROUP
    middle = small + [((rows, A_COLS), bf16), ((rows, B_COLS), bf16), ((512, rows), bf16), ((1, rows), bf16)]
    final = small + [((2, rows, 256), bf16), ((2, rows, 512), bf16), ((512, rows), bf16), ((1, rows), bf16)]
    dma = pltpu.SemaphoreType.DMA
    held = pl.pallas_call(
        comm_kernel,
        out_shape=[jax.ShapeDtypeStruct(*s) for s in middle],
        in_specs=[pl.BlockSpec(memory_space=pl.ANY)] * 16,
        out_specs=[pl.BlockSpec(memory_space=pltpu.VMEM)] * 16,
        scratch_shapes=[
            pltpu.VMEM((4,) + qk, f32), pltpu.VMEM((4,) + vg, f32), pltpu.VMEM((4,) + o, f32), pltpu.VMEM((4,) + n, f32),
            pltpu.VMEM(qk, f32), pltpu.VMEM(vg, f32), pltpu.VMEM(o, f32),
            pltpu.VMEM((NX * NY, 1, 128), f32), pltpu.VMEM((NZ, 2, 128), f32),
            dma((16,)), dma((NX * NY - 1,)), dma((NX * NY - 1,)), dma((NZ - 1,)), dma((NZ - 1,)),
            dma((3,)), dma((3,)), dma((2, HALF)), dma((2, HALF)), dma((2, NZ)), dma((2, NZ)), dma((NZ,)), dma((NZ,)),
            dma((2, HALF, SUBS)), dma((2, HALF, SUBS))],
        compiler_params=pltpu.CompilerParams(collective_id=0, has_side_effects=True, vmem_limit_bytes=24 << 20),
        name="lamb_gather",
    )(*operands)
    outs = pl.pallas_call(
        store_kernel,
        out_shape=[jax.ShapeDtypeStruct(*s) for s in final],
        in_specs=[pl.BlockSpec(memory_space=pltpu.VMEM)] * 16,
        out_specs=[pl.BlockSpec(memory_space=pl.ANY)] * 16,
        scratch_shapes=[dma((18,))],
        compiler_params=pltpu.CompilerParams(vmem_limit_bytes=24 << 20),
        name="store",
    )(*held)
    outs = list(outs)
    for i in (0, 1, 2, 3, 4, 5, 12, 13, 14):
        outs[i] = outs[i][None]
    for i in (6, 7, 8):
        outs[i] = jnp.swapaxes(outs[i], 1, 2)
    return tuple(outs)


def solution(mesh):
    matrix = P("section", None, "shard", "tensor")
    across = P("section", "tensor", "shard")
    gain = P("section", "shard")
    return jax.shard_map(
        on_device,
        mesh=mesh,
        in_specs=(matrix,) * 8 + (across,) * 4 + (gain,) * 4,
        out_specs=(matrix,) * 6 + (across,) * 3 + (gain,) * 3
        + (P("section", None, None, "tensor"), P("section", None, None, "tensor"), P("section", "tensor", None), P("section", None)),
        check_vma=False,
    )
```

```python
import functools

import jax
import jax.numpy as jnp
from jax import lax
from jax.experimental import pallas as pl
from jax.experimental.pallas import tpu as pltpu
from jax.sharding import PartitionSpec as P

STEP = 10
BETA_ONE = 0.9
BETA_TWO = 0.999
EPSILON = 1e-06
LEARN_RATE = 0.2
FIRST_SCALE = 1.0 / (1.0 - BETA_ONE**STEP)
SECOND_SCALE = 1.0 / (1.0 - BETA_TWO**STEP)

MESH = pl.DeviceIdType.MESH
NX, NY, NZ = 4, 4, 16
HALF = NZ // 2
ROWS = 16
GROUP = NX * ROWS
A_COLS, B_COLS = 768, 1280
SUBS = 4
W_LANE, U_LANE = 64, 72
FAR_FIRST = sorted(range(1, NZ), key=lambda d: -min(d, NZ - d))
LAG = 1


def terms(p, g, m, s, decay):
    first = BETA_ONE * m + (1.0 - BETA_ONE) * g
    second = BETA_TWO * s + (1.0 - BETA_TWO) * g * g
    update = first * FIRST_SCALE / (jnp.sqrt(second * SECOND_SCALE) + EPSILON)
    if decay:
        update = update + decay * p
    return first, second, update


def total(v):
    return jnp.sum(jnp.sum(v, axis=0, keepdims=True), axis=1, keepdims=True)


def comm_kernel(*refs):
    (qk_p, qk_g, qk_m, qk_s, vg_p, vg_g, vg_m, vg_s, o_p, o_g, o_m, o_s, n_p, n_g, n_m, n_s) = refs[:16]
    (qk_new, qk_first, qk_second, vg_new, vg_first, vg_second, o_new, o_first, o_second,
     n_new, n_first, n_second, part_a, part_b, o_copy, n_copy) = refs[16:32]
    (b_qk, b_vg, b_o, b_n, u_qk, u_vg, u_o, slots_one, slots_two, load_sem, one_send, one_recv, two_send, two_recv,
     ax_send, ax_recv, bz_send, bz_recv, bx_send, bx_recv, br_send, br_recv, az_send, az_recv) = refs[32:]

    shard = lax.axis_index("shard")
    y = lax.axis_index("tensor")
    z = shard // NX
    x = shard % NX
    q = y * NX + x

    def at(dz=0, dx=0):
        return {"shard": ((z + dz + NZ) % NZ) * NX + (x + dx + NX) % NX}

    def at_plane(d):
        other = (q + d) % (NX * NY)
        return {"shard": z * NX + other % NX, "tensor": other // NX}

    def rows(dz=0, dx=0):
        return pl.multiple_of(((z + dz + NZ) % NZ) * GROUP + ((x + dx + NX) % NX) * ROWS, ROWS)

    barrier = pltpu.get_barrier_semaphore()
    for d in FAR_FIRST:
        pl.semaphore_signal(barrier, inc=1, device_id=at(dz=d), device_id_type=MESH)
    for d in range(1, NX * NY):
        pl.semaphore_signal(barrier, inc=1, device_id=at_plane(d), device_id_type=MESH)

    loads = []
    for i, (group, buffer) in enumerate((
        ((qk_p, qk_g, qk_m, qk_s), b_qk), ((vg_p, vg_g, vg_m, vg_s), b_vg),
        ((o_p, o_g, o_m, o_s), b_o), ((n_p, n_g, n_m, n_s), b_n))):
        for k, ref in enumerate(group):
            loads.append(pltpu.make_async_copy(ref, buffer.at[k], load_sem.at[4 * i + k]))
            loads[-1].start()

    lane = lax.broadcasted_iota(jnp.int32, (1, 128), 1)
    line = jnp.zeros((1, 128), jnp.float32)
    for k in range(4):
        loads[12 + k].wait()
    first, second, gain_update = terms(b_n[0], b_n[1], b_n[2], b_n[3], 0.0)
    n_first[...] = first
    n_second[...] = second
    slots_one[q] = line
    slots_one[q, :, 0:16] = b_n[0]
    slots_one[q, :, 16:32] = gain_update
    index = 0
    for i, (buffer, u_ref, first_ref, second_ref, count) in enumerate((
        (b_qk, u_qk, qk_first, qk_second, 2), (b_vg, u_vg, vg_first, vg_second, 2), (b_o, u_o, o_first, o_second, 1))):
        for k in range(4):
            loads[4 * i + k].wait()
        for k in range(count):
            p, g, m, s = (buffer[j, k] for j in range(4))
            first, second, update = terms(p, g, m, s, 0.01)
            first_ref[k] = first
            second_ref[k] = second
            u_ref[k] = update
            line = jnp.where(lane == W_LANE + index, total(p * p), line)
            line = jnp.where(lane == U_LANE + index, total(update * update), line)
            index += 1
    slots_one[q] = slots_one[q] + line

    pl.semaphore_wait(barrier, NX * NY - 1 + NZ - 1)
    sends = []
    one = []
    for d in range(1, NX * NY):
        one.append(pltpu.make_async_remote_copy(
            slots_one.at[q], slots_one.at[q], one_send.at[d - 1], one_recv.at[d - 1], device_id=at_plane(d), device_id_type=MESH))
        one[-1].start()
    for copy in one:
        copy.wait_recv()
    sends += one
    plane = slots_one[0]
    for d in range(1, NX * NY):
        plane = plane + slots_one[d]
    gains = jnp.zeros((1, 128), jnp.float32)
    for k in range(NX):
        gain_line = jnp.where(lane < 32, slots_one[y * NX + k], 0.0)
        gains = gains + (pltpu.roll(gain_line, 32 * k, 1) if k else gain_line)
    slots_two[z, 0:1] = plane
    slots_two[z, 1:2] = gains
    two = []
    for d in FAR_FIRST:
        two.append(pltpu.make_async_remote_copy(
            slots_two.at[z], slots_two.at[z], two_send.at[d - 1], two_recv.at[d - 1], device_id=at(dz=d), device_id_type=MESH))
        two[-1].start()
    for copy in two:
        copy.wait_recv()
    sends += two
    sums = slots_two[0, 0:1]
    for d in range(1, NZ):
        sums = sums + slots_two[d, 0:1]
    roots = jnp.sqrt(jnp.where(lane >= W_LANE, sums, 0.0))
    ratio = LEARN_RATE * (roots / (pltpu.roll(roots, 128 - (U_LANE - W_LANE), 1) + EPSILON))
    rate = [jnp.sum(jnp.where(lane == W_LANE + i, ratio, 0.0), axis=1, keepdims=True) for i in range(5)]

    mine = rows()
    new = b_vg[0, 0] - rate[2] * u_vg[0]
    vg_new[0] = new
    part_b[pl.ds(mine, ROWS), 0:512] = new.astype(jnp.bfloat16)
    new = b_vg[0, 1] - rate[3] * u_vg[1]
    vg_new[1] = new
    part_b[pl.ds(mine, ROWS), 512:1024] = new.astype(jnp.bfloat16)
    new = b_qk[0, 1] - rate[1] * u_qk[1]
    qk_new[1] = new
    part_b[pl.ds(mine, ROWS), 1024:1280] = new.astype(jnp.bfloat16)

    def send(ref, start, size, send_sem, recv_sem, target):
        block = ref.at[pl.ds(start, size)]
        copy = pltpu.make_async_remote_copy(block, block, send_sem, recv_sem, device_id=target, device_id_type=MESH)
        copy.start()
        sends.append(copy)
        return copy

    SIDE = (1, -1)
    STEPS = (HALF, HALF - 1)

    def send_bz(side, k):
        return send(part_b, rows(dz=-SIDE[side] * k), ROWS, bz_send.at[side, k], bz_recv.at[side, k], at(dz=SIDE[side]))

    def send_bx(j, dz):
        return [send(part_b, rows(dz=dz), ROWS, bx_send.at[side, j], bx_recv.at[side, j], at(dx=SIDE[side])) for side in range(2)]

    def relay_bx(j, dz):
        side = j % 2
        across[j][side].wait_recv()
        return send(part_b, rows(dz=dz, dx=-SIDE[side]), ROWS, br_send.at[j], br_recv.at[j], at(dx=SIDE[side]))

    PIECE = GROUP // SUBS

    def subs_of(side, k):
        if k < HALF - 1:
            return range(SUBS)
        return range(SUBS // 2) if side == 0 else range(SUBS // 2, SUBS)

    def send_az(side, k, h):
        dz = -SIDE[side] * k
        start = pl.multiple_of(((z + dz + NZ) % NZ) * GROUP + h * PIECE, PIECE)
        return send(part_a, start, PIECE, az_send.at[side, k, h], az_recv.at[side, k, h], at(dz=SIDE[side]))

    bz = [[send_bz(0, 0)], [send_bz(1, 0)]]
    new = b_o[0, 0] - rate[4] * u_o[0]
    o_new[0] = new
    part_a[pl.ds(mine, ROWS), 0:512] = new.astype(jnp.bfloat16)
    new = b_qk[0, 0] - rate[0] * u_qk[0]
    qk_new[0] = new
    part_a[pl.ds(mine, ROWS), 512:768] = new.astype(jnp.bfloat16)
    ax = [send(part_a, mine, ROWS, ax_send.at[d - 1], ax_recv.at[d - 1], at(dx=d)) for d in (1, 3, 2)]
    across = {0: send_bx(0, 0)}
    relays = {}
    where = {0: 0}

    lanes = lax.broadcasted_iota(jnp.int32, (NZ, 128), 1)
    held = jnp.concatenate([slots_two[d, 1:2] for d in range(NZ)], axis=0)
    valid = lanes % 32 < 16
    gain = jnp.where(valid, held, 0.0)
    update = jnp.where(valid, pltpu.roll(held, 128 - 16, 1), 0.0)
    gain_rate = LEARN_RATE * (jnp.sqrt(total(gain * gain)) / (jnp.sqrt(total(update * update)) + EPSILON))
    n_new[...] = b_n[0] - gain_rate * gain_update
    gain = gain - gain_rate * update
    packed = jnp.where(lanes < 16, gain, 0.0)
    for k in range(1, NX):
        packed = packed + jnp.where((lanes >= 16 * k) & (lanes < 16 * k + 16), pltpu.roll(gain, 128 - 16 * k, 1), 0.0)
    moved = pltpu.roll(packed, 64, 1)
    for d in range(HALF):
        n_copy[:, 128 * d : 128 * d + 128] = (packed[2 * d : 2 * d + 1] + moved[2 * d + 1 : 2 * d + 2]).astype(jnp.bfloat16)

    def transpose_pair(i):
        start = pl.multiple_of((z // 2 + i + HALF) % HALF * 128, 128)
        block = part_a[pl.ds(start, 128), 0:512].astype(jnp.float32)
        o_copy[:, pl.ds(start, 128)] = block.T.astype(jnp.bfloat16)

    az = [{}, {}]

    def az_step(k):
        if k == 0:
            for copy in ax:
                copy.wait_recv()
        for h in range(SUBS):
            for side in range(2):
                if k:
                    if h in subs_of(side, k - 1):
                        az[side][k - 1, h].wait_recv()
                if k < HALF and h in subs_of(side, k):
                    az[side][k, h] = send_az(side, k, h)
        if k == HALF:
            transpose_pair(HALF // 2)
        elif k % 2 == 1:
            i = (k - 1) // 2
            transpose_pair(-i)
            if i:
                transpose_pair(i)

    for k in range(HALF + max(LAG, 1) + 1):
        if k < HALF:
            for side in range(2):
                if k < STEPS[side]:
                    bz[side][k].wait_recv()
                    if k + 1 < STEPS[side]:
                        bz[side].append(send_bz(side, k + 1))
                    j = 1 + 2 * k + side
                    where[j] = -SIDE[side] * (k + 1)
                    across[j] = send_bx(j, where[j])
        if k >= LAG and k - LAG <= HALF:
            az_step(k - LAG)
        for j in ((0,) if k == 0 else (2 * k - 1, 2 * k)):
            if j < NZ:
                relays[j] = relay_bx(j, where[j])
    for j in range(NZ):
        across[j][1 - j % 2].wait_recv()
        relays[j].wait_recv()
    for copy in sends:
        copy.wait_send()


def store_kernel(*refs):
    (qk_new, qk_first, qk_second, vg_new, vg_first, vg_second, o_new, o_first, o_second,
     n_new, n_first, n_second, part_a, part_b, o_copy, n_copy) = refs[:16]
    outs = refs[16:32]
    sem = refs[32]
    pairs = [
        (part_b.at[:, 0:512], outs[13].at[0]), (part_b.at[:, 512:1024], outs[13].at[1]), (o_copy, outs[14]),
        (part_a.at[:, 512:768], outs[12].at[0]), (part_b.at[:, 1024:1280], outs[12].at[1]),
        *zip(refs[:12], outs[:12]), (n_copy, outs[15])]
    copies = [pltpu.make_async_copy(source, target, sem.at[i]) for i, (source, target) in enumerate(pairs)]
    for copy in copies:
        copy.start()
    for copy in copies:
        copy.wait()


def on_device(*args):
    f32, bf16 = jnp.float32, jnp.bfloat16
    operands = []
    for i, array in enumerate(args):
        if i < 8:
            operands.append(array.reshape(array.shape[1:]))
        elif i < 12:
            operands.append(jnp.swapaxes(array, 1, 2))
        else:
            operands.append(array)
    qk, vg, o, n = (operands[4 * i].shape for i in range(4))
    small = [(qk, f32)] * 3 + [(vg, f32)] * 3 + [(o, f32)] * 3 + [(n, f32)] * 3
    rows = NZ * GROUP
    middle = small + [((rows, A_COLS), bf16), ((rows, B_COLS), bf16), ((512, rows), bf16), ((1, rows), bf16)]
    final = small + [((2, rows, 256), bf16), ((2, rows, 512), bf16), ((512, rows), bf16), ((1, rows), bf16)]
    dma = pltpu.SemaphoreType.DMA
    held = pl.pallas_call(
        comm_kernel,
        out_shape=[jax.ShapeDtypeStruct(*s) for s in middle],
        in_specs=[pl.BlockSpec(memory_space=pl.ANY)] * 16,
        out_specs=[pl.BlockSpec(memory_space=pltpu.VMEM)] * 16,
        scratch_shapes=[
            pltpu.VMEM((4,) + qk, f32), pltpu.VMEM((4,) + vg, f32), pltpu.VMEM((4,) + o, f32), pltpu.VMEM((4,) + n, f32),
            pltpu.VMEM(qk, f32), pltpu.VMEM(vg, f32), pltpu.VMEM(o, f32),
            pltpu.VMEM((NX * NY, 1, 128), f32), pltpu.VMEM((NZ, 2, 128), f32),
            dma((16,)), dma((NX * NY - 1,)), dma((NX * NY - 1,)), dma((NZ - 1,)), dma((NZ - 1,)),
            dma((3,)), dma((3,)), dma((2, HALF)), dma((2, HALF)), dma((2, NZ)), dma((2, NZ)), dma((NZ,)), dma((NZ,)),
            dma((2, HALF, SUBS)), dma((2, HALF, SUBS))],
        compiler_params=pltpu.CompilerParams(collective_id=0, has_side_effects=True, vmem_limit_bytes=24 << 20),
        name="lamb_gather",
    )(*[pltpu.with_memory_space_constraint(a, pltpu.HBM) for a in operands])
    outs = pl.pallas_call(
        store_kernel,
        out_shape=[jax.ShapeDtypeStruct(*s) for s in final],
        in_specs=[pl.BlockSpec(memory_space=pltpu.VMEM)] * 16,
        out_specs=[pl.BlockSpec(memory_space=pl.ANY)] * 16,
        scratch_shapes=[dma((18,))],
        compiler_params=pltpu.CompilerParams(vmem_limit_bytes=24 << 20),
        name="store",
    )(*held)
    outs = list(outs)
    for i in (0, 1, 2, 3, 4, 5, 12, 13, 14):
        outs[i] = outs[i][None]
    for i in (6, 7, 8):
        outs[i] = jnp.swapaxes(outs[i], 1, 2)
    return tuple(outs)


def solution(mesh):
    matrix = P("section", None, "shard", "tensor")
    across = P("section", "tensor", "shard")
    gain = P("section", "shard")
    return jax.shard_map(
        on_device,
        mesh=mesh,
        in_specs=(matrix,) * 8 + (across,) * 4 + (gain,) * 4,
        out_specs=(matrix,) * 6 + (across,) * 3 + (gain,) * 3
        + (P("section", None, None, "tensor"), P("section", None, None, "tensor"), P("section", "tensor", None), P("section", None)),
        check_vma=False,
    )
```
